32 devices in a mesh: image: 4 (over y, x), space: 8 (over z, core).
Axes of the slice: x: 2, y: 2, z: 4, core: 2. Of those that a mesh axis runs over, the one named last changes fastest.
Arguments:
- displacement: float32 [4, 3, 8192], P('image', None, 'space'), may hold values from -0.5 to 0.5
- end_states: float32 [2, 3, 8192], P(None, None, 'space'), may hold values from -0.5 to 0.5
- atom_live: int32 [8192], P('space'), may hold values 0 or 1
- partner_cells: int32 [64, 5], P('space'), may hold values from 0 to 11, as said below
- partner_live: int32 [64, 5], P('space'), may hold values from 0 to 1
- spring_const: float32 [4], P('image'), may hold values from 2 to 20
Outputs:
- band_force: float32 [4, 3, 8192], P('image', None, 'space')
- path_stats: float32 [4, 3], P('image')
The draws below stay inside these ranges and needn't reach their ends.
Inputs may be any that keep to these rules, and one draw needn't show every extreme that they name: `partner_cells`: each cell's live entries name the cell itself (index c + 2), the cells c + 1 and c + 3, and for some cells c or c + 4; the live entries are symmetric between cells of the image (counting cells modulo 64); entries come in any order and dead entries name arbitrary cells.
All inputs are finite; a program needn't handle non-finite values. No bound on the sum of `atom_live` on one device may be relied on, other than what follows from the above.
Results may differ from the reference program's by a relative error of at most 0.0003.
Values sent between devices are 32-bit elements; how exact they have to be, the bound alone decides.
A program may use at most 64 MiB of HBM per device.

```python
import math
import jax
import jax.numpy as jnp
from jax import lax

CELLS = 8
SLOTS = 128
GHOST = 2
ITERATIONS = 6
IMAGES = 4
ALL_CELLS = 64
ATOMS = 8192
N_SPACE = 8


def partner_tables(key):
    cell_ids = jnp.arange(CELLS * N_SPACE, dtype=jnp.int32)
    total_cells = CELLS * N_SPACE
    links = jax.random.randint(jax.random.fold_in(key, 11), (total_cells,), 0, 2).astype(jnp.int32)
    local_ids = cell_ids % CELLS
    offsets = jnp.array([-2, -1, 0, 1, 2], jnp.int32)
    entries = local_ids[:, None] + GHOST + offsets[None, :]
    upper = links[cell_ids]
    lower = links[(cell_ids - 2) % total_cells]
    steady = jnp.ones((total_cells,), jnp.int32)
    used = jnp.stack([lower, steady, steady, steady, upper], axis=1)
    random_cells = jax.random.randint(jax.random.fold_in(key, 12), (total_cells, 5), 0, CELLS + 2 * GHOST).astype(jnp.int32)
    entries = jnp.where(used == 1, entries, random_cells)
    scores = jax.random.randint(jax.random.fold_in(key, 13), (total_cells, 5), 0, 1 << 20).astype(jnp.int32) * 5 + jnp.arange(5, dtype=jnp.int32)[None, :]
    order = jnp.argsort(scores, axis=1)
    entries = jnp.take_along_axis(entries, order, axis=1)
    used = jnp.take_along_axis(used, order, axis=1)
    return (entries.astype(jnp.int32), used.astype(jnp.int32))


def draw_partner_cells(key, part):
    return partner_tables(key)[0]


def draw_partner_live(key, part):
    return partner_tables(key)[1]


def touch_ends(values, stream_key, low, top_value):
    place = [jax.random.randint(jax.random.fold_in(stream_key, axis), (), 0, length) for axis, length in enumerate(values.shape)]
    widest = values.shape.index(max(values.shape))
    beside = place[:widest] + [(place[widest] + 1) % values.shape[widest]] + place[widest + 1:]
    return values.at[tuple(place)].set(low).at[tuple(beside)].set(top_value)


def level_of(own_key, extent, shards, low, high):
    def one(dim, parts):
        steps = jax.random.uniform(jax.random.fold_in(jax.random.fold_in(own_key, 6), dim), (parts,), jnp.float32, low / len(shards), high / len(shards))
        return jnp.repeat(jnp.exp(steps), extent[dim] // parts).reshape((-1,) + (1,) * (len(extent) - dim - 1))

    loudness = one(*shards[0])
    for cut in shards[1:]:
        loudness = loudness * one(*cut)
    return loudness


def gaussian(rng, shape, deviation, bound, shards=(), kind=jnp.bfloat16):
    values = deviation * jax.random.normal(rng, shape, jnp.float32)
    if shards:
        values = values * level_of(rng, shape, shards, -0.22, 0.18)
    return jnp.clip(values, -bound, bound).astype(kind)


def setup_inputs(seed: int = 0) -> dict:
    streams_of = jax.random.split(jax.random.key(seed), 7)
    displacement = gaussian(streams_of[0], (IMAGES, 3, ATOMS), 0.1, 0.5, ((0, 4), (2, 8)), jnp.float32)
    end_states = gaussian(streams_of[1], (2, 3, ATOMS), 0.1, 0.5, ((2, 8),), jnp.float32)
    atom_live = touch_ends((jax.random.randint(streams_of[2], (ATOMS,), 0, 8) < 7).astype(jnp.int32), jax.random.fold_in(streams_of[2], 1), 0, 1)
    partner_cells = draw_partner_cells(jax.random.fold_in(streams_of[6], 71), 0)
    partner_live = draw_partner_live(jax.random.fold_in(streams_of[6], 71), 0)
    spring_const = jnp.clip(jnp.exp(math.log(20.0) - 2.3025851 * jax.random.uniform(streams_of[5], (IMAGES,), jnp.float32) ** level_of(streams_of[5], (IMAGES,), ((0, 4),), -0.2, 0.2)), 2.0, 20.0)
    return dict(displacement=displacement, end_states=end_states, atom_live=atom_live, partner_cells=partner_cells, partner_live=partner_live, spring_const=spring_const)


cutoff_sq = 9.0
pair_strength = 0.4
step_size = 0.02
epsilon = 1e-06
ref_block = 8

def site_table():
    slot_ids = jnp.arange(SLOTS, dtype=jnp.int32)
    return jnp.stack([slot_ids // 64, slot_ids // 8 % 8, slot_ids % 8]).astype(jnp.float32)

def tile_weight(own_live, partner_atoms, tile_live, self_tile, partner):
    diagonal = jnp.arange(SLOTS, dtype=jnp.int32)[:, None] == jnp.arange(SLOTS, dtype=jnp.int32)[None, :]
    weight = own_live[:, :, None] * partner_atoms[:, partner, None, :] * tile_live[:, partner, None, None]
    return jnp.where(self_tile[:, partner, None, None] & diagonal[None], jnp.float32(0.0), weight)

def pair_geometry(own_sites, partner_sites, partner):
    separation = own_sites[:, :, :, None] - partner_sites[:, partner, :, None, :]
    scaled = lax.optimization_barrier(jnp.sum(separation * separation, axis=1)) / cutoff_sq
    remain = jnp.where(scaled < 1.0, 1.0 - scaled, jnp.float32(0.0))
    return (separation, remain)

def density_cells(own_sites, partner_sites, own_live, partner_atoms, tile_live, self_tile):
    density = jnp.zeros(own_live.shape, jnp.float32)
    for partner in range(partner_sites.shape[1]):
        separation, remain = pair_geometry(own_sites, partner_sites, partner)
        weight = tile_weight(own_live, partner_atoms, tile_live, self_tile, partner)
        density = density + lax.optimization_barrier(jnp.sum(weight * remain ** 4, axis=-1))
    return density

def force_cells(own_sites, partner_sites, own_live, partner_atoms, tile_live, self_tile, own_slope, partner_slope):
    total = jnp.zeros(own_sites.shape, jnp.float32)
    for partner in range(partner_sites.shape[1]):
        separation, remain = pair_geometry(own_sites, partner_sites, partner)
        weight = tile_weight(own_live, partner_atoms, tile_live, self_tile, partner)
        slopes = own_slope[:, :, None] + partner_slope[:, partner, None, :]
        coefficient = slopes * (-4.0 * remain ** 3) + pair_strength * (-3.0 * remain ** 2)
        total = total + lax.optimization_barrier(jnp.sum((weight * coefficient)[:, None] * separation, axis=-1))
    return -(2.0 / cutoff_sq) * total

def blocked(function, block_cells, *arrays):
    total_rows = arrays[0].shape[0]
    shaped = tuple((item.reshape((total_rows // block_cells, block_cells) + item.shape[1:]) for item in arrays))
    result = lax.map(lambda group: function(*group), shaped)
    return result.reshape((total_rows,) + result.shape[2:])

def image_forces(moved, live_cells, partner_cells, tile_live):
    cell_disp = moved.reshape(3, ALL_CELLS, SLOTS).transpose(1, 0, 2)
    cell_ids = jnp.arange(ALL_CELLS, dtype=jnp.int32)
    local_ids = cell_ids % CELLS
    targets = (cell_ids[:, None] - local_ids[:, None] + partner_cells - GHOST) % ALL_CELLS
    site = site_table()
    axis_unit = jnp.array([1.0, 0.0, 0.0], jnp.float32)
    own_offset = (2 * (local_ids + GHOST)).astype(jnp.float32)[:, None, None] * axis_unit[None, :, None]
    own_sites = cell_disp + site[None] + own_offset
    part_offset = (2 * partner_cells).astype(jnp.float32)[:, :, None, None] * axis_unit[None, None, :, None]
    partner_sites = cell_disp[targets] + site[None, None] + part_offset
    partner_atoms = live_cells[targets]
    self_tile = partner_cells == (local_ids + GHOST)[:, None]
    density = blocked(density_cells, ref_block, own_sites, partner_sites, live_cells, partner_atoms, tile_live, self_tile)
    slope = -0.5 / jnp.sqrt(1.0 + density) * live_cells
    partner_slope = slope[targets]
    force = blocked(force_cells, ref_block, own_sites, partner_sites, live_cells, partner_atoms, tile_live, self_tile, slope, partner_slope)
    return force.transpose(1, 0, 2).reshape(3, ATOMS)

def reference(displacement, end_states, atom_live, partner_cells, partner_live, spring_const):
    live_flat = atom_live.astype(jnp.float32)
    live_cells = live_flat.reshape(ALL_CELLS, SLOTS)
    tile_live = partner_live.astype(jnp.float32)
    moved = displacement
    for iteration in range(ITERATIONS):
        previous = jnp.concatenate([end_states[0:1], moved[:-1]], axis=0)
        following = jnp.concatenate([moved[1:], end_states[1:2]], axis=0)
        forward_gap = (following - moved) * live_flat
        backward_gap = (moved - previous) * live_flat
        force = lax.map(lambda item: image_forces(item, live_cells, partner_cells, tile_live), moved)
        forward_sq = lax.optimization_barrier(jnp.sum(forward_gap * forward_gap, axis=(1, 2)))
        backward_sq = lax.optimization_barrier(jnp.sum(backward_gap * backward_gap, axis=(1, 2)))
        cross_sum = lax.optimization_barrier(jnp.sum(forward_gap * backward_gap, axis=(1, 2)))
        force_ahead = lax.optimization_barrier(jnp.sum(force * forward_gap, axis=(1, 2)))
        force_behind = lax.optimization_barrier(jnp.sum(force * backward_gap, axis=(1, 2)))
        length_ahead = jnp.sqrt(forward_sq + epsilon)
        length_behind = jnp.sqrt(backward_sq + epsilon)
        tangent_sq = forward_sq / length_ahead ** 2 + backward_sq / length_behind ** 2 + 2.0 * cross_sum / (length_ahead * length_behind)
        tangent_len = jnp.sqrt(jnp.maximum(tangent_sq, 1.0))
        tangent = (forward_gap / length_ahead[:, None, None] + backward_gap / length_behind[:, None, None]) / tangent_len[:, None, None]
        parallel = (force_ahead / length_ahead + force_behind / length_behind) / tangent_len
        spring_term = spring_const * (length_ahead - length_behind)
        band_force = force + (spring_term - parallel)[:, None, None] * tangent
        cosine = cross_sum / (length_ahead * length_behind)
        path_stats = jnp.stack([parallel, spring_term, cosine], axis=-1)
        moved = moved + step_size * band_force
    return (band_force, path_stats)
```

```python
import functools

import jax
import jax.numpy as jnp
from jax import lax
from jax.experimental import pallas as pl
from jax.experimental.pallas import tpu as pltpu
from jax.sharding import PartitionSpec as P

LANES = 128
GHOST = 2
ITERATIONS = 6
RADIUS = 3.0
STEP = 0.02
EPS = 1e-6
FAR = 1.0e4
SPAN = 2 * GHOST + 1
ROWS = 32
ONES = 21
PROWS = 8


def parts(v):
    high = v.astype(jnp.bfloat16).astype(jnp.float32)
    rest = v - high
    mid = rest.astype(jnp.bfloat16).astype(jnp.float32)
    return high, mid, rest - mid


def fold(v):
    return jnp.sum(v, axis=(0, 1))[None]


def kernel(
    n, ni, cells,
    data, out,
    wide, live_wide, left_rows, right_rows, pleft, pright,
    flat, turned, pturned, tiles, density, moment,
    halo, usend, urecv, gsend, grecv, fsend, frecv, asend, arecv, bsend, brecv,
    hs, hr, us, ur, gs, gr, fs, fr, as_, ar, bs, br,
):
    ext = 3 * cells
    me = lax.axis_index("space")
    im = lax.axis_index("image")
    right, left = lax.rem(me + 1, n), lax.rem(me + n - 1, n)
    down, up = lax.rem(im + 1, ni), lax.rem(im + ni - 1, ni)

    def sp(d):
        return {"space": d}

    barrier = pltpu.get_barrier_semaphore()
    for d in range(1, n):
        pl.semaphore_signal(barrier, inc=1, device_id=sp(lax.rem(me + d, n)))
    for d in (up, down):
        pl.semaphore_signal(barrier, inc=1, device_id={"image": d})
    pl.semaphore_wait(barrier, n + 1)

    def remote(src, dst, ssem, rsem, dev):
        return pltpu.make_async_remote_copy(
            src_ref=src, dst_ref=dst, send_sem=ssem, recv_sem=rsem,
            device_id=dev, device_id_type=pl.DeviceIdType.MESH,
        )

    first = [
        remote(data.at[pl.ds(0, 5)], halo.at[0], hs.at[0], hr.at[0], sp(right)),
        remote(data.at[pl.ds(0, 5)], halo.at[1], hs.at[1], hr.at[1], sp(left)),
    ]
    for c in first:
        c.start()

    cell_id = lax.broadcasted_iota(jnp.int32, (ext, LANES), 0)
    slot = lax.broadcasted_iota(jnp.int32, (ext, LANES), 1)
    site = [
        (slot // 64 + 2 * cell_id - ext).astype(jnp.float32),
        (slot // 8 % 8).astype(jnp.float32) - 3.5,
        (slot % 8).astype(jnp.float32) - 3.5,
    ]
    one = jnp.ones((ext, LANES), jnp.float32)
    zero = jnp.zeros((ext, LANES), jnp.float32)

    def put(ref, row, v):
        ref[pl.ds(row * ext, ext), :] = v

    for r in range(3):
        put(left_rows, ONES + r, one)
        put(right_rows, ONES - 3 + r, one)
    for r in range(ONES + 3 + SPAN, ROWS):
        put(left_rows, r, zero)
        put(right_rows, r, zero)
    for r in range(PROWS):
        put(pleft, r, one if 3 <= r < 6 else zero)
        put(pright, r, one if r < 3 else zero)
    for r in range(SPAN):
        put(left_rows, ONES + 3 + r, jnp.where(cell_id % SPAN == r, one, zero))
    density[...] = zero
    for c in first:
        c.wait()
    for k in range(3):
        wide[k, pl.ds(0, cells), :] = halo[0, k]
        wide[k, pl.ds(cells, cells), :] = data[k]
        wide[k, pl.ds(2 * cells, cells), :] = halo[1, k]
    live_wide[pl.ds(0, cells), :] = halo[0, 3]
    live_wide[pl.ds(cells, cells), :] = data[3]
    live_wide[pl.ds(2 * cells, cells), :] = halo[1, 3]
    used = jnp.concatenate([halo[0, 4], data[4], halo[1, 4]], axis=0)
    bars = [
        jnp.broadcast_to((used[:, o : o + 1] - 1.0) * FAR, (ext, LANES)) for o in range(SPAN)
    ]
    for r in range(SPAN):
        bar = zero
        for o in range(SPAN):
            bar = jnp.where((cell_id + (o + SPAN - GHOST)) % SPAN == r, bars[o], bar)
        put(right_rows, ONES + 3 + r, bar)

    low = cells - 2 * GHOST
    diagonal = lax.broadcasted_iota(jnp.int32, (LANES, LANES), 0) == lax.broadcasted_iota(
        jnp.int32, (LANES, LANES), 1
    )
    spring_const = data[11]
    own = pl.ds(cells, cells)

    def step(it, carry):
        par = lax.rem(it, 2)
        for k in range(3):
            usend[par, k] = wide[k, own, :]
        ucopy = [
            remote(usend.at[par], urecv.at[par, 0], us.at[par, 0], ur.at[par, 0], {"image": down}),
            remote(usend.at[par], urecv.at[par, 1], us.at[par, 1], ur.at[par, 1], {"image": up}),
        ]
        for c in ucopy:
            c.start()

        live = live_wide[...]
        place = [(wide[k] + site[k]) * (1.0 / RADIUS) for k in range(3)]
        for k in range(3):
            h, m, l = parts(place[k])
            for j, v in enumerate((h, h, m, m, h, l)):
                put(left_rows, 6 * k + j, v)
            h, m, l = 2.0 * h, 2.0 * m, 2.0 * l
            for j, v in enumerate((h, m, h, m, l, h)):
                put(right_rows, 6 * k + j, v)
        square = place[0] * place[0] + place[1] * place[1] + place[2] * place[2]
        q = 0.5 - square + (live - 1.0) * FAR
        for j, v in enumerate(parts(q)):
            put(left_rows, ONES - 3 + j, v)
            put(right_rows, ONES + j, v)

        for e in range(low, ext - low):
            block = left_rows[pl.ds(e, ROWS, stride=ext), :]
            flat[:, pl.ds(e * LANES, LANES)] = block.astype(jnp.bfloat16)
            turned[pl.ds((e - low) * LANES, LANES), :] = block.T.astype(jnp.bfloat16)

        for c in range(cells - GHOST, 2 * cells + GHOST):
            near = right_rows[pl.ds(c, ROWS, stride=ext), :].astype(jnp.bfloat16)
            t = jnp.dot(
                turned[pl.ds((c - GHOST - low) * LANES, SPAN * LANES), :], near,
                preferred_element_type=jnp.float32,
            )
            t = jnp.maximum(t, 0.0)
            a, b = GHOST * LANES, (GHOST + 1) * LANES
            t = jnp.concatenate([t[:a], jnp.where(diagonal, 0.0, t[a:b]), t[b:]], axis=0)
            if cells <= c < 2 * cells:
                tiles[c - cells] = t
            s = t * t
            s = s * s
            density[pl.ds(c, 1), :] = jnp.sum(s, axis=0, keepdims=True)

        for c in ucopy:
            c.wait_recv()
        own_live = live_wide[own, :]
        ahead, behind = [], []
        for k in range(3):
            mine = wide[k, own, :]
            prev = jnp.where(im == 0, data[5 + k], urecv[par, 0, k])
            nxt = jnp.where(im == ni - 1, data[8 + k], urecv[par, 1, k])
            ahead.append((nxt - mine) * own_live)
            behind.append((mine - prev) * own_live)
            gsend[par, k] = ahead[k]
            gsend[par, 3 + k] = behind[k]
        gcopy = [
            remote(gsend.at[par], grecv.at[par, 0], gs.at[par, 0], gr.at[par, 0], sp(right)),
            remote(gsend.at[par], grecv.at[par, 1], gs.at[par, 1], gr.at[par, 1], sp(left)),
        ]
        for c in gcopy:
            c.start()

        def lanes(x, y):
            v = x[0] * y[0] + x[1] * y[1] + x[2] * y[2]
            return jnp.sum(v, axis=0, keepdims=True)

        def spread(send, recv, ssem, rsem, rows):
            for j, v in enumerate(rows):
                send[par, pl.ds(j, 1), :] = v
                recv[par, me, pl.ds(j, 1), :] = v
            copies = []
            for d in range(1, n):
                copies.append(
                    remote(
                        send.at[par], recv.at[par, me], ssem.at[par, d], rsem.at[par, d],
                        sp(lax.rem(me + d, n)),
                    )
                )
                copies[-1].start()
            return copies

        acopy = spread(
            asend, arecv, as_, ar,
            [lanes(ahead, ahead), lanes(behind, behind), lanes(ahead, behind), own_live[:1]],
        )

        steep = 2.0 * live / jnp.sqrt(1.0 + density[...])
        for j, v in enumerate(parts(steep)):
            put(pleft, j, v)
            put(pright, 3 + j, v)
        for e in range(cells - GHOST, 2 * cells + GHOST):
            block = pleft[pl.ds(e, PROWS, stride=ext), :]
            pturned[pl.ds((e - cells + GHOST) * LANES, LANES), :] = block.T.astype(jnp.bfloat16)
        for c in range(cells):
            near = pright[pl.ds(c + cells, PROWS, stride=ext), :].astype(jnp.bfloat16)
            both = jnp.dot(
                pturned[pl.ds(c * LANES, SPAN * LANES), :], near,
                preferred_element_type=jnp.float32,
            )
            t = tiles[c]
            pull = (t * t) * (both * t - 1.2)
            high = pull.astype(jnp.bfloat16)
            rest = (pull - high.astype(jnp.float32)).astype(jnp.bfloat16)
            x = flat[:, pl.ds((c + cells - GHOST) * LANES, SPAN * LANES)]
            v = jnp.dot(x, high, preferred_element_type=jnp.float32) + jnp.dot(
                x, rest, preferred_element_type=jnp.float32
            )
            for k in range(3):
                moment[k, pl.ds(c, 1), :] = (
                    v[6 * k : 6 * k + 1] + v[6 * k + 2 : 6 * k + 3] + v[6 * k + 5 : 6 * k + 6]
                )
            moment[3, pl.ds(c, 1), :] = v[ONES : ONES + 1]

        total = moment[3]
        force = [
            (moment[k] - place[k][cells : 2 * cells] * total) * (2.0 / RADIUS) for k in range(3)
        ]
        for k in range(3):
            fsend[par, k] = force[k]
        bcopy = spread(bsend, brecv, bs, br, [lanes(force, ahead), lanes(force, behind)])
        fcopy = [
            remote(fsend.at[par], frecv.at[par, 0], fs.at[par, 0], fr.at[par, 0], sp(right)),
            remote(fsend.at[par], frecv.at[par, 1], fs.at[par, 1], fr.at[par, 1], sp(left)),
        ]
        for c in fcopy:
            c.start()

        for c in acopy:
            c.wait_recv()
        sums = jnp.sum(jnp.sum(arecv[par], axis=0), axis=-1, keepdims=True)
        aa, bb, ab = sums[0:1], sums[1:2], sums[2:3]
        la, lb = jnp.sqrt(aa + EPS), jnp.sqrt(bb + EPS)
        cosine = ab / (la * lb)
        norm = jnp.sqrt(jnp.maximum(aa / (la * la) + bb / (lb * lb) + 2.0 * cosine, 1.0))
        ga, gb = 1.0 / (la * norm), 1.0 / (lb * norm)
        spring = spring_const[0:1] * (la - lb)
        for c in gcopy:
            c.wait_recv()
        for c in fcopy:
            c.wait_recv()
        for c in bcopy:
            c.wait_recv()
        sums = jnp.sum(jnp.sum(brecv[par], axis=0), axis=-1, keepdims=True)
        parallel = sums[0:1] * ga + sums[1:2] * gb
        gain = spring - parallel
        ga, gb = gain * ga, gain * gb
        for k in range(3):
            band = force[k] + (ahead[k] * ga + behind[k] * gb)
            out[k] = band
            wide[k, own, :] = wide[k, own, :] + STEP * band
            for side in range(2):
                where = pl.ds(2 * cells * side, cells)
                band = frecv[par, side, k] + (
                    grecv[par, side, k] * ga + grecv[par, side, 3 + k] * gb
                )
                wide[k, where, :] = wide[k, where, :] + STEP * band
        out[3, pl.ds(0, 1), :] = jnp.broadcast_to(parallel, (1, LANES))
        out[3, pl.ds(1, 1), :] = jnp.broadcast_to(spring, (1, LANES))
        out[3, pl.ds(2, 1), :] = jnp.broadcast_to(cosine, (1, LANES))
        for c in ucopy + gcopy + acopy + bcopy + fcopy:
            c.wait_send()
        return carry

    out[3] = jnp.zeros((cells, LANES), jnp.float32)
    lax.fori_loop(0, ITERATIONS, step, 0)


def solution(mesh):
    n, ni = mesh.shape["space"], mesh.shape["image"]

    def body(displacement, end_states, atom_live, partner_cells, partner_live, spring_const):
        cells = partner_cells.shape[0]
        own = jnp.arange(cells, dtype=jnp.int32)[:, None, None]
        offset = jnp.arange(LANES, dtype=jnp.int32)[None, None, :]
        hit = (partner_cells[:, :, None] == own + offset) & (partner_live[:, :, None] > 0)
        used = jnp.any(hit, axis=1).astype(jnp.float32)
        data = jnp.concatenate(
            [
                displacement.reshape(3, cells, LANES),
                atom_live.astype(jnp.float32).reshape(1, cells, LANES),
                used[None],
                end_states.reshape(6, cells, LANES),
                jnp.broadcast_to(spring_const[:, None, None], (1, cells, LANES)),
            ],
            axis=0,
        )
        ext = 3 * cells
        f32, bf16 = jnp.float32, jnp.bfloat16
        sem = pltpu.SemaphoreType.DMA
        V = pltpu.VMEM
        inner = cells + 2 * GHOST
        out = pl.pallas_call(
            functools.partial(kernel, n, ni, cells),
            out_shape=jax.ShapeDtypeStruct((4, cells, LANES), f32),
            in_specs=[pl.BlockSpec(memory_space=pltpu.VMEM)],
            out_specs=pl.BlockSpec(memory_space=pltpu.VMEM),
            scratch_shapes=[
                V((3, ext, LANES), f32),
                V((ext, LANES), f32),
                V((ROWS * ext, LANES), f32),
                V((ROWS * ext, LANES), f32),
                V((PROWS * ext, LANES), f32),
                V((PROWS * ext, LANES), f32),
                V((ROWS, ext * LANES), bf16),
                V(((inner + 2 * GHOST) * LANES, ROWS), bf16),
                V((inner * LANES, PROWS), bf16),
                V((cells, SPAN * LANES, LANES), f32),
                V((ext, LANES), f32),
                V((4, cells, LANES), f32),
                V((2, 5, cells, LANES), f32),
                V((2, 3, cells, LANES), f32),
                V((2, 2, 3, cells, LANES), f32),
                V((2, 6, cells, LANES), f32),
                V((2, 2, 6, cells, LANES), f32),
                V((2, 3, cells, LANES), f32),
                V((2, 2, 3, cells, LANES), f32),
                V((2, 4, LANES), f32),
                V((2, n, 4, LANES), f32),
                V((2, 2, LANES), f32),
                V((2, n, 2, LANES), f32),
                sem((2,)), sem((2,)),
                sem((2, 2)), sem((2, 2)),
                sem((2, 2)), sem((2, 2)),
                sem((2, 2)), sem((2, 2)),
                sem((2, n)), sem((2, n)),
                sem((2, n)), sem((2, n)),
            ],
            compiler_params=pltpu.CompilerParams(collective_id=0, has_side_effects=True),
        )(data)
        return out[:3].reshape(1, 3, -1), out[3, :3, 0][None]

    return jax.shard_map(
        body,
        mesh=mesh,
        in_specs=(
            P("image", None, "space"),
            P(None, None, "space"),
            P("space"),
            P("space", None),
            P("space", None),
            P("image"),
        ),
        out_specs=(P("image", None, "space"), P("image", None)),
        check_vma=False,
    )
```

```python
import functools

import jax
import jax.numpy as jnp
from jax import lax
from jax.experimental import pallas as pl
from jax.experimental.pallas import tpu as pltpu
from jax.sharding import PartitionSpec as P

LANES = 128
GHOST = 2
ITERATIONS = 6
RADIUS = 3.0
STEP = 0.02
EPS = 1e-6
FAR = 1.0e4
SPAN = 2 * GHOST + 1
ROWS = 32
ONES = 21
PROWS = 8


def parts(v):
    high = v.astype(jnp.bfloat16).astype(jnp.float32)
    rest = v - high
    mid = rest.astype(jnp.bfloat16).astype(jnp.float32)
    return high, mid, rest - mid


def fold(v):
    return jnp.sum(v, axis=(0, 1))[None]


def kernel(
    n, ni, cells,
    data, out,
    wide, live_wide, left_rows, right_rows, pleft, pright,
    flat, turned, pturned, tiles, density, moment,
    halo, usend, urecv, gsend, grecv, fsend, frecv, asend, arecv, bsend, brecv,
    hs, hr, us, ur, gs, gr, fs, fr, as_, ar, bs, br,
):
    ext = 3 * cells
    me = lax.axis_index("space")
    im = lax.axis_index("image")
    right, left = lax.rem(me + 1, n), lax.rem(me + n - 1, n)
    down, up = lax.rem(im + 1, ni), lax.rem(im + ni - 1, ni)

    def sp(d):
        return {"space": d}

    barrier = pltpu.get_barrier_semaphore()
    for d in range(1, n):
        pl.semaphore_signal(barrier, inc=1, device_id=sp(lax.rem(me + d, n)))
    for d in (up, down):
        pl.semaphore_signal(barrier, inc=1, device_id={"image": d})

    def remote(src, dst, ssem, rsem, dev):
        return pltpu.make_async_remote_copy(
            src_ref=src, dst_ref=dst, send_sem=ssem, recv_sem=rsem,
            device_id=dev, device_id_type=pl.DeviceIdType.MESH,
        )

    first = [
        remote(data.at[pl.ds(0, 5)], halo.at[0], hs.at[0], hr.at[0], sp(right)),
        remote(data.at[pl.ds(0, 5)], halo.at[1], hs.at[1], hr.at[1], sp(left)),
    ]

    cell_id = lax.broadcasted_iota(jnp.int32, (ext, LANES), 0)
    slot = lax.broadcasted_iota(jnp.int32, (ext, LANES), 1)
    site = [
        (slot // 64 + 2 * cell_id - ext).astype(jnp.float32),
        (slot // 8 % 8).astype(jnp.float32) - 3.5,
        (slot % 8).astype(jnp.float32) - 3.5,
    ]
    one = jnp.ones((ext, LANES), jnp.float32)
    zero = jnp.zeros((ext, LANES), jnp.float32)

    def put(ref, row, v):
        ref[pl.ds(row * ext, ext), :] = v

    for r in range(3):
        put(left_rows, ONES + r, one)
        put(right_rows, ONES - 3 + r, one)
    for r in range(ONES + 3 + SPAN, ROWS):
        put(left_rows, r, zero)
        put(right_rows, r, zero)
    for r in range(PROWS):
        put(pleft, r, one if 3 <= r < 6 else zero)
        put(pright, r, one if r < 3 else zero)
    for r in range(SPAN):
        put(left_rows, ONES + 3 + r, jnp.where(cell_id % SPAN == r, one, zero))
    density[...] = zero
    pl.semaphore_wait(barrier, n + 1)
    for c in first:
        c.start()
    for c in first:
        c.wait()
    for k in range(3):
        wide[k, pl.ds(0, cells), :] = halo[0, k]
        wide[k, pl.ds(cells, cells), :] = data[k]
        wide[k, pl.ds(2 * cells, cells), :] = halo[1, k]
    live_wide[pl.ds(0, cells), :] = halo[0, 3]
    live_wide[pl.ds(cells, cells), :] = data[3]
    live_wide[pl.ds(2 * cells, cells), :] = halo[1, 3]
    used = jnp.concatenate([halo[0, 4], data[4], halo[1, 4]], axis=0)
    bars = [
        jnp.broadcast_to((used[:, o : o + 1] - 1.0) * FAR, (ext, LANES)) for o in range(SPAN)
    ]
    for r in range(SPAN):
        bar = zero
        for o in range(SPAN):
            bar = jnp.where((cell_id + (o + SPAN - GHOST)) % SPAN == r, bars[o], bar)
        put(right_rows, ONES + 3 + r, bar)

    low = cells - 2 * GHOST
    diagonal = lax.broadcasted_iota(jnp.int32, (LANES, LANES), 0) == lax.broadcasted_iota(
        jnp.int32, (LANES, LANES), 1
    )
    spring_const = data[11]
    own = pl.ds(cells, cells)

    def step(it, carry):
        par = lax.rem(it, 2)
        for k in range(3):
            usend[par, k] = wide[k, own, :]
        ucopy = [
            remote(usend.at[par], urecv.at[par, 0], us.at[par, 0], ur.at[par, 0], {"image": down}),
            remote(usend.at[par], urecv.at[par, 1], us.at[par, 1], ur.at[par, 1], {"image": up}),
        ]
        for c in ucopy:
            c.start()

        live = live_wide[...]
        place = [(wide[k] + site[k]) * (1.0 / RADIUS) for k in range(3)]
        for k in range(3):
            h, m, l = parts(place[k])
            for j, v in enumerate((h, h, m, m, h, l)):
                put(left_rows, 6 * k + j, v)
            h, m, l = 2.0 * h, 2.0 * m, 2.0 * l
            for j, v in enumerate((h, m, h, m, l, h)):
                put(right_rows, 6 * k + j, v)
        square = place[0] * place[0] + place[1] * place[1] + place[2] * place[2]
        q = 0.5 - square + (live - 1.0) * FAR
        for j, v in enumerate(parts(q)):
            put(left_rows, ONES - 3 + j, v)
            put(right_rows, ONES + j, v)

        for e in range(low, ext - low):
            block = left_rows[pl.ds(e, ROWS, stride=ext), :]
            flat[:, pl.ds(e * LANES, LANES)] = block.astype(jnp.bfloat16)
            turned[pl.ds((e - low) * LANES, LANES), :] = block.T.astype(jnp.bfloat16)

        for c in range(cells - GHOST, 2 * cells + GHOST):
            near = right_rows[pl.ds(c, ROWS, stride=ext), :].astype(jnp.bfloat16)
            t = jnp.dot(
                turned[pl.ds((c - GHOST - low) * LANES, SPAN * LANES), :], near,
                preferred_element_type=jnp.float32,
            )
            t = jnp.maximum(t, 0.0)
            a, b = GHOST * LANES, (GHOST + 1) * LANES
            t = jnp.concatenate([t[:a], jnp.where(diagonal, 0.0, t[a:b]), t[b:]], axis=0)
            if cells <= c < 2 * cells:
                tiles[c - cells] = t
            s = t * t
            s = s * s
            density[pl.ds(c, 1), :] = jnp.sum(s, axis=0, keepdims=True)

        def lanes(x, y):
            v = x[0] * y[0] + x[1] * y[1] + x[2] * y[2]
            return jnp.sum(v, axis=0, keepdims=True)

        def spread(send, recv, ssem, rsem, rows):
            for j, v in enumerate(rows):
                send[par, pl.ds(j, 1), :] = v
                recv[par, me, pl.ds(j, 1), :] = v
            copies = []
            for d in range(1, n):
                copies.append(
                    remote(
                        send.at[par], recv.at[par, me], ssem.at[par, d], rsem.at[par, d],
                        sp(lax.rem(me + d, n)),
                    )
                )
                copies[-1].start()
            return copies

        steep = 2.0 * live / jnp.sqrt(1.0 + density[...])
        for j, v in enumerate(parts(steep)):
            put(pleft, j, v)
            put(pright, 3 + j, v)
        for e in range(cells - GHOST, 2 * cells + GHOST):
            block = pleft[pl.ds(e, PROWS, stride=ext), :]
            pturned[pl.ds((e - cells + GHOST) * LANES, LANES), :] = block.T.astype(jnp.bfloat16)
        for c in range(cells):
            if c == cells - 2:
                for copy in ucopy:
                    copy.wait_recv()
                own_live = live_wide[own, :]
                ahead, behind = [], []
                for k in range(3):
                    mine = wide[k, own, :]
                    prev = jnp.where(im == 0, data[5 + k], urecv[par, 0, k])
                    nxt = jnp.where(im == ni - 1, data[8 + k], urecv[par, 1, k])
                    ahead.append((nxt - mine) * own_live)
                    behind.append((mine - prev) * own_live)
                    gsend[par, k] = ahead[k]
                    gsend[par, 3 + k] = behind[k]
                gcopy = [
                    remote(gsend.at[par], grecv.at[par, 0], gs.at[par, 0], gr.at[par, 0], sp(right)),
                    remote(gsend.at[par], grecv.at[par, 1], gs.at[par, 1], gr.at[par, 1], sp(left)),
                ]
                for copy in gcopy:
                    copy.start()

                acopy = spread(
                    asend, arecv, as_, ar,
                    [lanes(ahead, ahead), lanes(behind, behind), lanes(ahead, behind), own_live[:1]],
                )
            near = pright[pl.ds(c + cells, PROWS, stride=ext), :].astype(jnp.bfloat16)
            both = jnp.dot(
                pturned[pl.ds(c * LANES, SPAN * LANES), :], near,
                preferred_element_type=jnp.float32,
            )
            t = tiles[c]
            pull = (t * t) * (both * t - 1.2)
            high = pull.astype(jnp.bfloat16)
            rest = (pull - high.astype(jnp.float32)).astype(jnp.bfloat16)
            x = flat[:, pl.ds((c + cells - GHOST) * LANES, SPAN * LANES)]
            v = jnp.dot(x, high, preferred_element_type=jnp.float32) + jnp.dot(
                x, rest, preferred_element_type=jnp.float32
            )
            for k in range(3):
                moment[k, pl.ds(c, 1), :] = (
                    v[6 * k : 6 * k + 1] + v[6 * k + 2 : 6 * k + 3] + v[6 * k + 5 : 6 * k + 6]
                )
            moment[3, pl.ds(c, 1), :] = v[ONES : ONES + 1]

        total = moment[3]
        force = [
            (moment[k] - place[k][cells : 2 * cells] * total) * (2.0 / RADIUS) for k in range(3)
        ]
        for k in range(3):
            fsend[par, k] = force[k]
        bcopy = spread(bsend, brecv, bs, br, [lanes(force, ahead), lanes(force, behind)])
        fcopy = [
            remote(fsend.at[par], frecv.at[par, 0], fs.at[par, 0], fr.at[par, 0], sp(right)),
            remote(fsend.at[par], frecv.at[par, 1], fs.at[par, 1], fr.at[par, 1], sp(left)),
        ]
        for c in fcopy:
            c.start()

        for c in acopy:
            c.wait_recv()
        sums = jnp.sum(jnp.sum(arecv[par], axis=0), axis=-1, keepdims=True)
        aa, bb, ab = sums[0:1], sums[1:2], sums[2:3]
        la, lb = jnp.sqrt(aa + EPS), jnp.sqrt(bb + EPS)
        cosine = ab / (la * lb)
        norm = jnp.sqrt(jnp.maximum(aa / (la * la) + bb / (lb * lb) + 2.0 * cosine, 1.0))
        ga, gb = 1.0 / (la * norm), 1.0 / (lb * norm)
        spring = spring_const[0:1] * (la - lb)
        for c in gcopy:
            c.wait_recv()
        for c in fcopy:
            c.wait_recv()
        for c in bcopy:
            c.wait_recv()
        sums = jnp.sum(jnp.sum(brecv[par], axis=0), axis=-1, keepdims=True)
        parallel = sums[0:1] * ga + sums[1:2] * gb
        gain = spring - parallel
        ga, gb = gain * ga, gain * gb
        for k in range(3):
            band = force[k] + (ahead[k] * ga + behind[k] * gb)
            out[k] = band
            wide[k, own, :] = wide[k, own, :] + STEP * band
            for side in range(2):
                where = pl.ds(2 * cells * side, cells)
                band = frecv[par, side, k] + (
                    grecv[par, side, k] * ga + grecv[par, side, 3 + k] * gb
                )
                wide[k, where, :] = wide[k, where, :] + STEP * band
        out[3, pl.ds(0, 1), :] = jnp.broadcast_to(parallel, (1, LANES))
        out[3, pl.ds(1, 1), :] = jnp.broadcast_to(spring, (1, LANES))
        out[3, pl.ds(2, 1), :] = jnp.broadcast_to(cosine, (1, LANES))
        for c in ucopy + gcopy + acopy + bcopy + fcopy:
            c.wait_send()
        return carry

    out[3] = jnp.zeros((cells, LANES), jnp.float32)
    lax.fori_loop(0, ITERATIONS, step, 0)


def solution(mesh):
    n, ni = mesh.shape["space"], mesh.shape["image"]

    def body(displacement, end_states, atom_live, partner_cells, partner_live, spring_const):
        cells = partner_cells.shape[0]
        own = jnp.arange(cells, dtype=jnp.int32)[:, None, None]
        offset = jnp.arange(LANES, dtype=jnp.int32)[None, None, :]
        hit = (partner_cells[:, :, None] == own + offset) & (partner_live[:, :, None] > 0)
        used = jnp.any(hit, axis=1).astype(jnp.float32)
        data = jnp.concatenate(
            [
                displacement.reshape(3, cells, LANES),
                atom_live.astype(jnp.float32).reshape(1, cells, LANES),
                used[None],
                end_states.reshape(6, cells, LANES),
                jnp.broadcast_to(spring_const[:, None, None], (1, cells, LANES)),
            ],
            axis=0,
        )
        ext = 3 * cells
        f32, bf16 = jnp.float32, jnp.bfloat16
        sem = pltpu.SemaphoreType.DMA
        V = pltpu.VMEM
        inner = cells + 2 * GHOST
        out = pl.pallas_call(
            functools.partial(kernel, n, ni, cells),
            out_shape=jax.ShapeDtypeStruct((4, cells, LANES), f32),
            in_specs=[pl.BlockSpec(memory_space=pltpu.VMEM)],
            out_specs=pl.BlockSpec(memory_space=pltpu.VMEM),
            scratch_shapes=[
                V((3, ext, LANES), f32),
                V((ext, LANES), f32),
                V((ROWS * ext, LANES), f32),
                V((ROWS * ext, LANES), f32),
                V((PROWS * ext, LANES), f32),
                V((PROWS * ext, LANES), f32),
                V((ROWS, ext * LANES), bf16),
                V(((inner + 2 * GHOST) * LANES, ROWS), bf16),
                V((inner * LANES, PROWS), bf16),
                V((cells, SPAN * LANES, LANES), f32),
                V((ext, LANES), f32),
                V((4, cells, LANES), f32),
                V((2, 5, cells, LANES), f32),
                V((2, 3, cells, LANES), f32),
                V((2, 2, 3, cells, LANES), f32),
                V((2, 6, cells, LANES), f32),
                V((2, 2, 6, cells, LANES), f32),
                V((2, 3, cells, LANES), f32),
                V((2, 2, 3, cells, LANES), f32),
                V((2, 4, LANES), f32),
                V((2, n, 4, LANES), f32),
                V((2, 2, LANES), f32),
                V((2, n, 2, LANES), f32),
                sem((2,)), sem((2,)),
                sem((2, 2)), sem((2, 2)),
                sem((2, 2)), sem((2, 2)),
                sem((2, 2)), sem((2, 2)),
                sem((2, n)), sem((2, n)),
                sem((2, n)), sem((2, n)),
            ],
            compiler_params=pltpu.CompilerParams(collective_id=0, has_side_effects=True),
        )(data)
        return out[:3].reshape(1, 3, -1), out[3, :3, 0][None]

    return jax.shard_map(
        body,
        mesh=mesh,
        in_specs=(
            P("image", None, "space"),
            P(None, None, "space"),
            P("space"),
            P("space", None),
            P("space", None),
            P("image"),
        ),
        out_specs=(P("image", None, "space"), P("image", None)),
        check_vma=False,
    )
```

```python
import functools

import jax
import jax.numpy as jnp
from jax import lax
from jax.experimental import pallas as pl
from jax.experimental.pallas import tpu as pltpu
from jax.sharding import PartitionSpec as P

LANES = 128
GHOST = 2
ITERATIONS = 6
RADIUS = 3.0
STEP = 0.02
EPS = 1e-6
FAR = 1.0e4
SPAN = 2 * GHOST + 1
ROWS = 32
ONES = 21
PROWS = 8


def parts(v):
    high = v.astype(jnp.bfloat16).astype(jnp.float32)
    rest = v - high
    mid = rest.astype(jnp.bfloat16).astype(jnp.float32)
    return high, mid, rest - mid


def fold(v):
    return jnp.sum(v, axis=(0, 1))[None]


def kernel(
    n, ni, cells,
    disp, ends, atoms, pcells, plive, spring_ref, out, stats,
    data,
    wide, live_wide, left_rows, right_rows, pleft, pright,
    flat, turned, pturned, tiles, density, moment,
    halo, usend, urecv, gsend, grecv, fsend, frecv, asend, arecv, bsend, brecv,
    hs, hr, us, ur, gs, gr, fs, fr, as_, ar, bs, br,
):
    ext = 3 * cells
    me = lax.axis_index("space")
    im = lax.axis_index("image")
    right, left = lax.rem(me + 1, n), lax.rem(me + n - 1, n)
    down, up = lax.rem(im + 1, ni), lax.rem(im + ni - 1, ni)

    def sp(d):
        return {"space": d}

    barrier = pltpu.get_barrier_semaphore()
    for d in range(1, n):
        pl.semaphore_signal(barrier, inc=1, device_id=sp(lax.rem(me + d, n)))
    for d in (up, down):
        pl.semaphore_signal(barrier, inc=1, device_id={"image": d})

    def remote(src, dst, ssem, rsem, dev):
        return pltpu.make_async_remote_copy(
            src_ref=src, dst_ref=dst, send_sem=ssem, recv_sem=rsem,
            device_id=dev, device_id_type=pl.DeviceIdType.MESH,
        )

    for k in range(3):
        data[k] = disp[k]
        data[5 + k] = ends[k, pl.ds(0, cells, stride=2), :]
        data[8 + k] = ends[k, pl.ds(1, cells, stride=2), :]
    data[3] = atoms[...].astype(jnp.float32)
    lane = lax.broadcasted_iota(jnp.int32, (cells, LANES), 1)
    base = lax.broadcasted_iota(jnp.int32, (cells, SPAN), 0)
    use = jnp.zeros((cells, LANES), jnp.float32)
    for o in range(SPAN):
        hit = jnp.where((pcells[...] == base + o) & (plive[...] > 0), 1.0, 0.0)
        use = jnp.where(lane == o, jnp.max(hit, axis=1, keepdims=True), use)
    data[4] = use

    first = [
        remote(data.at[pl.ds(0, 5)], halo.at[0], hs.at[0], hr.at[0], sp(right)),
        remote(data.at[pl.ds(0, 5)], halo.at[1], hs.at[1], hr.at[1], sp(left)),
    ]

    cell_id = lax.broadcasted_iota(jnp.int32, (ext, LANES), 0)
    slot = lax.broadcasted_iota(jnp.int32, (ext, LANES), 1)
    site = [
        (slot // 64 + 2 * cell_id - ext).astype(jnp.float32),
        (slot // 8 % 8).astype(jnp.float32) - 3.5,
        (slot % 8).astype(jnp.float32) - 3.5,
    ]
    one = jnp.ones((ext, LANES), jnp.float32)
    zero = jnp.zeros((ext, LANES), jnp.float32)

    def put(ref, row, v):
        ref[pl.ds(row * ext, ext), :] = v

    for r in range(3):
        put(left_rows, ONES + r, one)
        put(right_rows, ONES - 3 + r, one)
    for r in range(ONES + 3 + SPAN, ROWS):
        put(left_rows, r, zero)
        put(right_rows, r, zero)
    for r in range(PROWS):
        put(pleft, r, one if 3 <= r < 6 else zero)
        put(pright, r, one if r < 3 else zero)
    for r in range(SPAN):
        put(left_rows, ONES + 3 + r, jnp.where(cell_id % SPAN == r, one, zero))
    density[...] = zero
    pl.semaphore_wait(barrier, n + 1)
    for c in first:
        c.start()
    for c in first:
        c.wait()
    for k in range(3):
        wide[k, pl.ds(0, cells), :] = halo[0, k]
        wide[k, pl.ds(cells, cells), :] = data[k]
        wide[k, pl.ds(2 * cells, cells), :] = halo[1, k]
    live_wide[pl.ds(0, cells), :] = halo[0, 3]
    live_wide[pl.ds(cells, cells), :] = data[3]
    live_wide[pl.ds(2 * cells, cells), :] = halo[1, 3]
    used = jnp.concatenate([halo[0, 4], data[4], halo[1, 4]], axis=0)
    bars = [
        jnp.broadcast_to((used[:, o : o + 1] - 1.0) * FAR, (ext, LANES)) for o in range(SPAN)
    ]
    for r in range(SPAN):
        bar = zero
        for o in range(SPAN):
            bar = jnp.where((cell_id + (o + SPAN - GHOST)) % SPAN == r, bars[o], bar)
        put(right_rows, ONES + 3 + r, bar)

    low = cells - 2 * GHOST
    diagonal = lax.broadcasted_iota(jnp.int32, (LANES, LANES), 0) == lax.broadcasted_iota(
        jnp.int32, (LANES, LANES), 1
    )
    spring_const = spring_ref[0]
    own = pl.ds(cells, cells)

    def step(it, carry):
        par = lax.rem(it, 2)
        for k in range(3):
            usend[par, k] = wide[k, own, :]
        ucopy = [
            remote(usend.at[par], urecv.at[par, 0], us.at[par, 0], ur.at[par, 0], {"image": down}),
            remote(usend.at[par], urecv.at[par, 1], us.at[par, 1], ur.at[par, 1], {"image": up}),
        ]
        for c in ucopy:
            c.start()

        live = live_wide[...]
        place = [(wide[k] + site[k]) * (1.0 / RADIUS) for k in range(3)]
        for k in range(3):
            h, m, l = parts(place[k])
            for j, v in enumerate((h, h, m, m, h, l)):
                put(left_rows, 6 * k + j, v)
            h, m, l = 2.0 * h, 2.0 * m, 2.0 * l
            for j, v in enumerate((h, m, h, m, l, h)):
                put(right_rows, 6 * k + j, v)
        square = place[0] * place[0] + place[1] * place[1] + place[2] * place[2]
        q = 0.5 - square + (live - 1.0) * FAR
        for j, v in enumerate(parts(q)):
            put(left_rows, ONES - 3 + j, v)
            put(right_rows, ONES + j, v)

        for e in range(low, ext - low):
            block = left_rows[pl.ds(e, ROWS, stride=ext), :]
            flat[:, pl.ds(e * LANES, LANES)] = block.astype(jnp.bfloat16)
            turned[pl.ds((e - low) * LANES, LANES), :] = block.T.astype(jnp.bfloat16)

        for c in range(cells - GHOST, 2 * cells + GHOST):
            near = right_rows[pl.ds(c, ROWS, stride=ext), :].astype(jnp.bfloat16)
            t = jnp.dot(
                turned[pl.ds((c - GHOST - low) * LANES, SPAN * LANES), :], near,
                preferred_element_type=jnp.float32,
            )
            t = jnp.maximum(t, 0.0)
            a, b = GHOST * LANES, (GHOST + 1) * LANES
            t = jnp.concatenate([t[:a], jnp.where(diagonal, 0.0, t[a:b]), t[b:]], axis=0)
            if cells <= c < 2 * cells:
                tiles[c - cells] = t
            s = t * t
            s = s * s
            density[pl.ds(c, 1), :] = jnp.sum(s, axis=0, keepdims=True)

        def lanes(x, y):
            v = x[0] * y[0] + x[1] * y[1] + x[2] * y[2]
            return jnp.sum(v, axis=0, keepdims=True)

        def spread(send, recv, ssem, rsem, rows):
            for j, v in enumerate(rows):
                send[par, pl.ds(j, 1), :] = v
                recv[par, me, pl.ds(j, 1), :] = v
            copies = []
            for d in range(1, n):
                copies.append(
                    remote(
                        send.at[par], recv.at[par, me], ssem.at[par, d], rsem.at[par, d],
                        sp(lax.rem(me + d, n)),
                    )
                )
                copies[-1].start()
            return copies

        steep = 2.0 * live / jnp.sqrt(1.0 + density[...])
        for j, v in enumerate(parts(steep)):
            put(pleft, j, v)
            put(pright, 3 + j, v)
        for e in range(cells - GHOST, 2 * cells + GHOST):
            block = pleft[pl.ds(e, PROWS, stride=ext), :]
            pturned[pl.ds((e - cells + GHOST) * LANES, LANES), :] = block.T.astype(jnp.bfloat16)
        for c in range(cells):
            if c == cells - 2:
                for copy in ucopy:
                    copy.wait_recv()
                own_live = live_wide[own, :]
                ahead, behind = [], []
                for k in range(3):
                    mine = wide[k, own, :]
                    prev = jnp.where(im == 0, data[5 + k], urecv[par, 0, k])
                    nxt = jnp.where(im == ni - 1, data[8 + k], urecv[par, 1, k])
                    ahead.append((nxt - mine) * own_live)
                    behind.append((mine - prev) * own_live)
                    gsend[par, k] = ahead[k]
                    gsend[par, 3 + k] = behind[k]
                gcopy = [
                    remote(gsend.at[par], grecv.at[par, 0], gs.at[par, 0], gr.at[par, 0], sp(right)),
                    remote(gsend.at[par], grecv.at[par, 1], gs.at[par, 1], gr.at[par, 1], sp(left)),
                ]
                for copy in gcopy:
                    copy.start()

                acopy = spread(
                    asend, arecv, as_, ar,
                    [lanes(ahead, ahead), lanes(behind, behind), lanes(ahead, behind), own_live[:1]],
                )
            near = pright[pl.ds(c + cells, PROWS, stride=ext), :].astype(jnp.bfloat16)
            both = jnp.dot(
                pturned[pl.ds(c * LANES, SPAN * LANES), :], near,
                preferred_element_type=jnp.float32,
            )
            t = tiles[c]
            pull = (t * t) * (both * t - 1.2)
            high = pull.astype(jnp.bfloat16)
            rest = (pull - high.astype(jnp.float32)).astype(jnp.bfloat16)
            x = flat[:, pl.ds((c + cells - GHOST) * LANES, SPAN * LANES)]
            v = jnp.dot(x, high, preferred_element_type=jnp.float32) + jnp.dot(
                x, rest, preferred_element_type=jnp.float32
            )
            for k in range(3):
                moment[k, pl.ds(c, 1), :] = (
                    v[6 * k : 6 * k + 1] + v[6 * k + 2 : 6 * k + 3] + v[6 * k + 5 : 6 * k + 6]
                )
            moment[3, pl.ds(c, 1), :] = v[ONES : ONES + 1]

        total = moment[3]
        force = [
            (moment[k] - place[k][cells : 2 * cells] * total) * (2.0 / RADIUS) for k in range(3)
        ]
        for k in range(3):
            fsend[par, k] = force[k]
        bcopy = spread(bsend, brecv, bs, br, [lanes(force, ahead), lanes(force, behind)])
        fcopy = [
            remote(fsend.at[par], frecv.at[par, 0], fs.at[par, 0], fr.at[par, 0], sp(right)),
            remote(fsend.at[par], frecv.at[par, 1], fs.at[par, 1], fr.at[par, 1], sp(left)),
        ]
        for c in fcopy:
            c.start()

        for c in acopy:
            c.wait_recv()
        sums = jnp.sum(jnp.sum(arecv[par], axis=0), axis=-1, keepdims=True)
        aa, bb, ab = sums[0:1], sums[1:2], sums[2:3]
        la, lb = jnp.sqrt(aa + EPS), jnp.sqrt(bb + EPS)
        cosine = ab / (la * lb)
        norm = jnp.sqrt(jnp.maximum(aa / (la * la) + bb / (lb * lb) + 2.0 * cosine, 1.0))
        ga, gb = 1.0 / (la * norm), 1.0 / (lb * norm)
        spring = spring_const * (la - lb)
        for c in gcopy:
            c.wait_recv()
        for c in fcopy:
            c.wait_recv()
        for c in bcopy:
            c.wait_recv()
        sums = jnp.sum(jnp.sum(brecv[par], axis=0), axis=-1, keepdims=True)
        parallel = sums[0:1] * ga + sums[1:2] * gb
        gain = spring - parallel
        ga, gb = gain * ga, gain * gb
        for k in range(3):
            band = force[k] + (ahead[k] * ga + behind[k] * gb)
            out[k] = band
            wide[k, own, :] = wide[k, own, :] + STEP * band
            for side in range(2):
                where = pl.ds(2 * cells * side, cells)
                band = frecv[par, side, k] + (
                    grecv[par, side, k] * ga + grecv[par, side, 3 + k] * gb
                )
                wide[k, where, :] = wide[k, where, :] + STEP * band
        stats[:, 0:1] = parallel
        stats[:, 1:2] = spring
        stats[:, 2:3] = cosine
        for c in ucopy + gcopy + acopy + bcopy + fcopy:
            c.wait_send()
        return carry

    lax.fori_loop(0, ITERATIONS, step, 0)


def solution(mesh):
    n, ni = mesh.shape["space"], mesh.shape["image"]

    def body(displacement, end_states, atom_live, partner_cells, partner_live, spring_const):
        cells = partner_cells.shape[0]
        ext = 3 * cells
        f32, bf16 = jnp.float32, jnp.bfloat16
        sem = pltpu.SemaphoreType.DMA
        V = pltpu.VMEM
        inner = cells + 2 * GHOST
        band, stats = pl.pallas_call(
            functools.partial(kernel, n, ni, cells),
            out_shape=(
                jax.ShapeDtypeStruct((3, cells, LANES), f32),
                jax.ShapeDtypeStruct((1, 3), f32),
            ),
            in_specs=[pl.BlockSpec(memory_space=pltpu.VMEM)] * 5
            + [pl.BlockSpec(memory_space=pltpu.SMEM)],
            out_specs=(pl.BlockSpec(memory_space=pltpu.VMEM),) * 2,
            scratch_shapes=[
                V((11, cells, LANES), f32),
                V((3, ext, LANES), f32),
                V((ext, LANES), f32),
                V((ROWS * ext, LANES), f32),
                V((ROWS * ext, LANES), f32),
                V((PROWS * ext, LANES), f32),
                V((PROWS * ext, LANES), f32),
                V((ROWS, ext * LANES), bf16),
                V(((inner + 2 * GHOST) * LANES, ROWS), bf16),
                V((inner * LANES, PROWS), bf16),
                V((cells, SPAN * LANES, LANES), f32),
                V((ext, LANES), f32),
                V((4, cells, LANES), f32),
                V((2, 5, cells, LANES), f32),
                V((2, 3, cells, LANES), f32),
                V((2, 2, 3, cells, LANES), f32),
                V((2, 6, cells, LANES), f32),
                V((2, 2, 6, cells, LANES), f32),
                V((2, 3, cells, LANES), f32),
                V((2, 2, 3, cells, LANES), f32),
                V((2, 4, LANES), f32),
                V((2, n, 4, LANES), f32),
                V((2, 2, LANES), f32),
                V((2, n, 2, LANES), f32),
                sem((2,)), sem((2,)),
                sem((2, 2)), sem((2, 2)),
                sem((2, 2)), sem((2, 2)),
                sem((2, 2)), sem((2, 2)),
                sem((2, n)), sem((2, n)),
                sem((2, n)), sem((2, n)),
            ],
            compiler_params=pltpu.CompilerParams(collective_id=0, has_side_effects=True),
        )(
            displacement.reshape(3, cells, LANES),
            end_states.reshape(2, 3, cells, LANES).transpose(1, 2, 0, 3).reshape(3, -1, LANES),
            atom_live.reshape(cells, LANES),
            partner_cells, partner_live, spring_const,
        )
        return band.reshape(1, 3, -1), stats

    return jax.shard_map(
        body,
        mesh=mesh,
        in_specs=(
            P("image", None, "space"),
            P(None, None, "space"),
            P("space"),
            P("space", None),
            P("space", None),
            P("image"),
        ),
        out_specs=(P("image", None, "space"), P("image", None)),
        check_vma=False,
    )
```

```python
import functools

import jax
import jax.numpy as jnp
from jax import lax
from jax.experimental import pallas as pl
from jax.experimental.pallas import tpu as pltpu
from jax.sharding import PartitionSpec as P

LANES = 128
GHOST = 2
ITERATIONS = 6
RADIUS = 3.0
STEP = 0.02
EPS = 1e-6
FAR = 1.0e4
SPAN = 2 * GHOST + 1
ROWS = 32
ONES = 21
PROWS = 8


def parts(v):
    high = v.astype(jnp.bfloat16).astype(jnp.float32)
    rest = v - high
    mid = rest.astype(jnp.bfloat16).astype(jnp.float32)
    return high, mid, rest - mid


def fold(v):
    return jnp.sum(v, axis=(0, 1))[None]


def kernel(
    n, ni, cells,
    disp, ends, atoms, pcells, plive, spring_ref, out, stats,
    data,
    wide, live_wide, left_rows, right_rows, pleft, pright,
    flat, turned, pturned, tiles, density, moment,
    halo, usend, urecv, gsend, grecv, fsend, frecv, asend, arecv, bsend, brecv,
    hs, hr, us, ur, gs, gr, fs, fr, as_, ar, bs, br,
):
    ext = 3 * cells
    me = lax.axis_index("space")
    im = lax.axis_index("image")
    right, left = lax.rem(me + 1, n), lax.rem(me + n - 1, n)
    down, up = lax.rem(im + 1, ni), lax.rem(im + ni - 1, ni)

    def sp(d):
        return {"space": d}

    barrier = pltpu.get_barrier_semaphore()
    for d in range(1, n):
        pl.semaphore_signal(barrier, inc=1, device_id=sp(lax.rem(me + d, n)))
    for d in (up, down):
        pl.semaphore_signal(barrier, inc=1, device_id={"image": d})

    def remote(src, dst, ssem, rsem, dev):
        return pltpu.make_async_remote_copy(
            src_ref=src, dst_ref=dst, send_sem=ssem, recv_sem=rsem,
            device_id=dev, device_id_type=pl.DeviceIdType.MESH,
        )

    for k in range(3):
        data[k] = disp[k]
        data[5 + k] = ends[k, pl.ds(0, cells, stride=2), :]
        data[8 + k] = ends[k, pl.ds(1, cells, stride=2), :]
    data[3] = atoms[...].astype(jnp.float32)
    lane = lax.broadcasted_iota(jnp.int32, (cells, LANES), 1)
    base = lax.broadcasted_iota(jnp.int32, (cells, SPAN), 0)
    use = jnp.zeros((cells, LANES), jnp.float32)
    for o in range(SPAN):
        hit = jnp.where((pcells[...] == base + o) & (plive[...] > 0), 1.0, 0.0)
        use = jnp.where(lane == o, jnp.max(hit, axis=1, keepdims=True), use)
    data[4] = use

    first = [
        remote(data, halo.at[0], hs.at[0], hr.at[0], sp(right)),
        remote(data, halo.at[1], hs.at[1], hr.at[1], sp(left)),
    ]

    cell_id = lax.broadcasted_iota(jnp.int32, (ext, LANES), 0)
    slot = lax.broadcasted_iota(jnp.int32, (ext, LANES), 1)
    site = [
        (slot // 64 + 2 * cell_id - ext).astype(jnp.float32),
        (slot // 8 % 8).astype(jnp.float32) - 3.5,
        (slot % 8).astype(jnp.float32) - 3.5,
    ]
    one = jnp.ones((ext, LANES), jnp.float32)
    zero = jnp.zeros((ext, LANES), jnp.float32)

    def put(ref, row, v):
        ref[pl.ds(row * ext, ext), :] = v

    for r in range(3):
        put(left_rows, ONES + r, one)
        put(right_rows, ONES - 3 + r, one)
    for r in range(ONES + 3 + SPAN, ROWS):
        put(left_rows, r, zero)
        put(right_rows, r, zero)
    for r in range(PROWS):
        put(pleft, r, one if 3 <= r < 6 else zero)
        put(pright, r, one if r < 3 else zero)
    for r in range(SPAN):
        put(left_rows, ONES + 3 + r, jnp.where(cell_id % SPAN == r, one, zero))
    density[...] = zero
    pl.semaphore_wait(barrier, n + 1)
    for c in first:
        c.start()
    for c in first:
        c.wait()
    for k in range(3):
        wide[k, pl.ds(0, cells), :] = halo[0, k]
        wide[k, pl.ds(cells, cells), :] = data[k]
        wide[k, pl.ds(2 * cells, cells), :] = halo[1, k]
    live_wide[pl.ds(0, cells), :] = halo[0, 3]
    live_wide[pl.ds(cells, cells), :] = data[3]
    live_wide[pl.ds(2 * cells, cells), :] = halo[1, 3]
    used = jnp.concatenate([halo[0, 4], data[4], halo[1, 4]], axis=0)
    bars = [
        jnp.broadcast_to((used[:, o : o + 1] - 1.0) * FAR, (ext, LANES)) for o in range(SPAN)
    ]
    for r in range(SPAN):
        bar = zero
        for o in range(SPAN):
            bar = jnp.where((cell_id + (o + SPAN - GHOST)) % SPAN == r, bars[o], bar)
        put(right_rows, ONES + 3 + r, bar)

    low = cells - 2 * GHOST
    diagonal = lax.broadcasted_iota(jnp.int32, (LANES, LANES), 0) == lax.broadcasted_iota(
        jnp.int32, (LANES, LANES), 1
    )
    spring_const = spring_ref[0]
    own = pl.ds(cells, cells)

    def step(it, carry):
        par = lax.rem(it, 2)
        for k in range(3):
            usend[par, k] = wide[k, own, :]
        ucopy = [
            remote(usend.at[par], urecv.at[par, 0], us.at[par, 0], ur.at[par, 0], {"image": down}),
            remote(usend.at[par], urecv.at[par, 1], us.at[par, 1], ur.at[par, 1], {"image": up}),
        ]
        for k in range(3):
            gsend[par, k] = wide[k, pl.ds(0, cells), :]
            gsend[par, 3 + k] = wide[k, pl.ds(2 * cells, cells), :]
        gcopy = [
            remote(gsend.at[par], grecv.at[par, 0], gs.at[par, 0], gr.at[par, 0], {"image": down}),
            remote(gsend.at[par], grecv.at[par, 1], gs.at[par, 1], gr.at[par, 1], {"image": up}),
        ]
        for c in ucopy + gcopy:
            c.start()

        live = live_wide[...]
        place = [(wide[k] + site[k]) * (1.0 / RADIUS) for k in range(3)]
        for k in range(3):
            h, m, l = parts(place[k])
            for j, v in enumerate((h, h, m, m, h, l)):
                put(left_rows, 6 * k + j, v)
            h, m, l = 2.0 * h, 2.0 * m, 2.0 * l
            for j, v in enumerate((h, m, h, m, l, h)):
                put(right_rows, 6 * k + j, v)
        square = place[0] * place[0] + place[1] * place[1] + place[2] * place[2]
        q = 0.5 - square + (live - 1.0) * FAR
        for j, v in enumerate(parts(q)):
            put(left_rows, ONES - 3 + j, v)
            put(right_rows, ONES + j, v)

        for e in range(low, ext - low):
            block = left_rows[pl.ds(e, ROWS, stride=ext), :]
            flat[:, pl.ds(e * LANES, LANES)] = block.astype(jnp.bfloat16)
            turned[pl.ds((e - low) * LANES, LANES), :] = block.T.astype(jnp.bfloat16)

        for c in range(cells - GHOST, 2 * cells + GHOST):
            near = right_rows[pl.ds(c, ROWS, stride=ext), :].astype(jnp.bfloat16)
            t = jnp.dot(
                turned[pl.ds((c - GHOST - low) * LANES, SPAN * LANES), :], near,
                preferred_element_type=jnp.float32,
            )
            t = jnp.maximum(t, 0.0)
            a, b = GHOST * LANES, (GHOST + 1) * LANES
            t = jnp.concatenate([t[:a], jnp.where(diagonal, 0.0, t[a:b]), t[b:]], axis=0)
            if cells <= c < 2 * cells:
                tiles[c - cells] = t
            s = t * t
            s = s * s
            density[pl.ds(c, 1), :] = jnp.sum(s, axis=0, keepdims=True)

        def lanes(x, y):
            v = x[0] * y[0] + x[1] * y[1] + x[2] * y[2]
            return jnp.sum(v, axis=0, keepdims=True)

        def spread(send, recv, ssem, rsem, rows):
            for j, v in enumerate(rows):
                send[par, pl.ds(j, 1), :] = v
                recv[par, me, pl.ds(j, 1), :] = v
            copies = []
            for d in range(1, n):
                copies.append(
                    remote(
                        send.at[par], recv.at[par, me], ssem.at[par, d], rsem.at[par, d],
                        sp(lax.rem(me + d, n)),
                    )
                )
                copies[-1].start()
            return copies

        steep = 2.0 * live / jnp.sqrt(1.0 + density[...])
        for j, v in enumerate(parts(steep)):
            put(pleft, j, v)
            put(pright, 3 + j, v)
        for e in range(cells - GHOST, 2 * cells + GHOST):
            block = pleft[pl.ds(e, PROWS, stride=ext), :]
            pturned[pl.ds((e - cells + GHOST) * LANES, LANES), :] = block.T.astype(jnp.bfloat16)
        for c in range(cells):
            if c == cells - 1:
                for copy in ucopy:
                    copy.wait_recv()
                own_live = live_wide[own, :]
                ahead, behind = [], []
                for k in range(3):
                    mine = wide[k, own, :]
                    prev = jnp.where(im == 0, data[5 + k], urecv[par, 0, k])
                    nxt = jnp.where(im == ni - 1, data[8 + k], urecv[par, 1, k])
                    ahead.append((nxt - mine) * own_live)
                    behind.append((mine - prev) * own_live)
                acopy = spread(
                    asend, arecv, as_, ar,
                    [lanes(ahead, ahead), lanes(behind, behind), lanes(ahead, behind), own_live[:1]],
                )
            near = pright[pl.ds(c + cells, PROWS, stride=ext), :].astype(jnp.bfloat16)
            both = jnp.dot(
                pturned[pl.ds(c * LANES, SPAN * LANES), :], near,
                preferred_element_type=jnp.float32,
            )
            t = tiles[c]
            pull = (t * t) * (both * t - 1.2)
            high = pull.astype(jnp.bfloat16)
            rest = (pull - high.astype(jnp.float32)).astype(jnp.bfloat16)
            x = flat[:, pl.ds((c + cells - GHOST) * LANES, SPAN * LANES)]
            v = jnp.dot(x, high, preferred_element_type=jnp.float32) + jnp.dot(
                x, rest, preferred_element_type=jnp.float32
            )
            for k in range(3):
                moment[k, pl.ds(c, 1), :] = (
                    v[6 * k : 6 * k + 1] + v[6 * k + 2 : 6 * k + 3] + v[6 * k + 5 : 6 * k + 6]
                )
            moment[3, pl.ds(c, 1), :] = v[ONES : ONES + 1]

        total = moment[3]
        force = [
            (moment[k] - place[k][cells : 2 * cells] * total) * (2.0 / RADIUS) for k in range(3)
        ]
        for k in range(3):
            fsend[par, k] = force[k]
        bcopy = spread(bsend, brecv, bs, br, [lanes(force, ahead), lanes(force, behind)])
        fcopy = [
            remote(fsend.at[par], frecv.at[par, 0], fs.at[par, 0], fr.at[par, 0], sp(right)),
            remote(fsend.at[par], frecv.at[par, 1], fs.at[par, 1], fr.at[par, 1], sp(left)),
        ]
        for c in fcopy:
            c.start()

        for c in acopy:
            c.wait_recv()
        sums = jnp.sum(jnp.sum(arecv[par], axis=0), axis=-1, keepdims=True)
        aa, bb, ab = sums[0:1], sums[1:2], sums[2:3]
        la, lb = jnp.sqrt(aa + EPS), jnp.sqrt(bb + EPS)
        cosine = ab / (la * lb)
        norm = jnp.sqrt(jnp.maximum(aa / (la * la) + bb / (lb * lb) + 2.0 * cosine, 1.0))
        ga, gb = 1.0 / (la * norm), 1.0 / (lb * norm)
        spring = spring_const * (la - lb)
        for c in gcopy:
            c.wait_recv()
        outer = []
        for side in range(2):
            where = pl.ds(2 * cells * side, cells)
            side_live = live_wide[where, :]
            for k in range(3):
                mine = wide[k, where, :]
                prev = jnp.where(im == 0, halo[side, 5 + k], grecv[par, 0, 3 * side + k])
                nxt = jnp.where(im == ni - 1, halo[side, 8 + k], grecv[par, 1, 3 * side + k])
                outer.append(((nxt - mine) * side_live, (mine - prev) * side_live))
        for c in fcopy:
            c.wait_recv()
        for c in bcopy:
            c.wait_recv()
        sums = jnp.sum(jnp.sum(brecv[par], axis=0), axis=-1, keepdims=True)
        parallel = sums[0:1] * ga + sums[1:2] * gb
        gain = spring - parallel
        ga, gb = gain * ga, gain * gb
        for k in range(3):
            band = force[k] + (ahead[k] * ga + behind[k] * gb)
            out[k] = band
            wide[k, own, :] = wide[k, own, :] + STEP * band
            for side in range(2):
                where = pl.ds(2 * cells * side, cells)
                gap = outer[3 * side + k]
                band = frecv[par, side, k] + (gap[0] * ga + gap[1] * gb)
                wide[k, where, :] = wide[k, where, :] + STEP * band
        stats[:, 0:1] = parallel
        stats[:, 1:2] = spring
        stats[:, 2:3] = cosine
        for c in ucopy + gcopy + acopy + bcopy + fcopy:
            c.wait_send()
        return carry

    lax.fori_loop(0, ITERATIONS, step, 0)


def solution(mesh):
    n, ni = mesh.shape["space"], mesh.shape["image"]

    def body(displacement, end_states, atom_live, partner_cells, partner_live, spring_const):
        cells = partner_cells.shape[0]
        ext = 3 * cells
        f32, bf16 = jnp.float32, jnp.bfloat16
        sem = pltpu.SemaphoreType.DMA
        V = pltpu.VMEM
        inner = cells + 2 * GHOST
        band, stats = pl.pallas_call(
            functools.partial(kernel, n, ni, cells),
            out_shape=(
                jax.ShapeDtypeStruct((3, cells, LANES), f32),
                jax.ShapeDtypeStruct((1, 3), f32),
            ),
            in_specs=[pl.BlockSpec(memory_space=pltpu.VMEM)] * 5
            + [pl.BlockSpec(memory_space=pltpu.SMEM)],
            out_specs=(pl.BlockSpec(memory_space=pltpu.VMEM),) * 2,
            scratch_shapes=[
                V((11, cells, LANES), f32),
                V((3, ext, LANES), f32),
                V((ext, LANES), f32),
                V((ROWS * ext, LANES), f32),
                V((ROWS * ext, LANES), f32),
                V((PROWS * ext, LANES), f32),
                V((PROWS * ext, LANES), f32),
                V((ROWS, ext * LANES), bf16),
                V(((inner + 2 * GHOST) * LANES, ROWS), bf16),
                V((inner * LANES, PROWS), bf16),
                V((cells, SPAN * LANES, LANES), f32),
                V((ext, LANES), f32),
                V((4, cells, LANES), f32),
                V((2, 11, cells, LANES), f32),
                V((2, 3, cells, LANES), f32),
                V((2, 2, 3, cells, LANES), f32),
                V((2, 6, cells, LANES), f32),
                V((2, 2, 6, cells, LANES), f32),
                V((2, 3, cells, LANES), f32),
                V((2, 2, 3, cells, LANES), f32),
                V((2, 4, LANES), f32),
                V((2, n, 4, LANES), f32),
                V((2, 2, LANES), f32),
                V((2, n, 2, LANES), f32),
                sem((2,)), sem((2,)),
                sem((2, 2)), sem((2, 2)),
                sem((2, 2)), sem((2, 2)),
                sem((2, 2)), sem((2, 2)),
                sem((2, n)), sem((2, n)),
                sem((2, n)), sem((2, n)),
            ],
            compiler_params=pltpu.CompilerParams(collective_id=0, has_side_effects=True),
        )(
            displacement.reshape(3, cells, LANES),
            end_states.reshape(2, 3, cells, LANES).transpose(1, 2, 0, 3).reshape(3, -1, LANES),
            atom_live.reshape(cells, LANES),
            partner_cells, partner_live, spring_const,
        )
        return band.reshape(1, 3, -1), stats

    return jax.shard_map(
        body,
        mesh=mesh,
        in_specs=(
            P("image", None, "space"),
            P(None, None, "space"),
            P("space"),
            P("space", None),
            P("space", None),
            P("image"),
        ),
        out_specs=(P("image", None, "space"), P("image", None)),
        check_vma=False,
    )
```

```python
import functools

import jax
import jax.numpy as jnp
from jax import lax
from jax.experimental import pallas as pl
from jax.experimental.pallas import tpu as pltpu
from jax.sharding import PartitionSpec as P

LANES = 128
GHOST = 2
ITERATIONS = 6
RADIUS = 3.0
STEP = 0.02
EPS = 1e-6
FAR = 1.0e4
SPAN = 2 * GHOST + 1
ROWS = 32
ONES = 21
PROWS = 8


def parts(v):
    high = v.astype(jnp.bfloat16).astype(jnp.float32)
    rest = v - high
    mid = rest.astype(jnp.bfloat16).astype(jnp.float32)
    return high, mid, rest - mid


def fold(v):
    return jnp.sum(v, axis=(0, 1))[None]


def kernel(
    n, ni, cells,
    disp, ends, atoms, pcells, plive, spring_ref, out, stats,
    data,
    wide, live_wide, left_rows, right_rows, pleft, pright,
    flat, turned, pturned, tiles, density, moment,
    halo, usend, urecv, gsend, grecv, fsend, frecv, asend, arecv, bsend, brecv,
    hs, hr, us, ur, gs, gr, fs, fr, as_, ar, bs, br,
):
    ext = 3 * cells
    me = lax.axis_index("space")
    im = lax.axis_index("image")
    right, left = lax.rem(me + 1, n), lax.rem(me + n - 1, n)
    down, up = lax.rem(im + 1, ni), lax.rem(im + ni - 1, ni)

    def sp(d):
        return {"space": d}

    barrier = pltpu.get_barrier_semaphore()
    for d in range(1, n):
        pl.semaphore_signal(barrier, inc=1, device_id=sp(lax.rem(me + d, n)))
    for d in (up, down):
        pl.semaphore_signal(barrier, inc=1, device_id={"image": d})

    def remote(src, dst, ssem, rsem, dev):
        return pltpu.make_async_remote_copy(
            src_ref=src, dst_ref=dst, send_sem=ssem, recv_sem=rsem,
            device_id=dev, device_id_type=pl.DeviceIdType.MESH,
        )

    for k in range(3):
        data[k] = disp[k]
        data[5 + k] = ends[k, pl.ds(0, cells, stride=2), :]
        data[8 + k] = ends[k, pl.ds(1, cells, stride=2), :]
    data[3] = atoms[...].astype(jnp.float32)
    lane = lax.broadcasted_iota(jnp.int32, (cells, LANES), 1)
    base = lax.broadcasted_iota(jnp.int32, (cells, SPAN), 0)
    use = jnp.zeros((cells, LANES), jnp.float32)
    for o in range(SPAN):
        hit = jnp.where((pcells[...] == base + o) & (plive[...] > 0), 1.0, 0.0)
        use = jnp.where(lane == o, jnp.max(hit, axis=1, keepdims=True), use)
    data[4] = use

    first = [
        remote(data.at[pl.ds(0, 5)], halo.at[0], hs.at[0], hr.at[0], sp(right)),
        remote(data.at[pl.ds(0, 5)], halo.at[1], hs.at[1], hr.at[1], sp(left)),
    ]

    cell_id = lax.broadcasted_iota(jnp.int32, (ext, LANES), 0)
    slot = lax.broadcasted_iota(jnp.int32, (ext, LANES), 1)
    site = [
        (slot // 64 + 2 * cell_id - ext).astype(jnp.float32),
        (slot // 8 % 8).astype(jnp.float32) - 3.5,
        (slot % 8).astype(jnp.float32) - 3.5,
    ]
    one = jnp.ones((ext, LANES), jnp.float32)
    zero = jnp.zeros((ext, LANES), jnp.float32)

    def put(ref, row, v):
        ref[pl.ds(row * ext, ext), :] = v

    for r in range(3):
        put(left_rows, ONES + r, one)
        put(right_rows, ONES - 3 + r, one)
    for r in range(ONES + 3 + SPAN, ROWS):
        put(left_rows, r, zero)
        put(right_rows, r, zero)
    for r in range(PROWS):
        put(pleft, r, one if 3 <= r < 6 else zero)
        put(pright, r, one if r < 3 else zero)
    for r in range(SPAN):
        put(left_rows, ONES + 3 + r, jnp.where(cell_id % SPAN == r, one, zero))
    density[...] = zero
    pl.semaphore_wait(barrier, n + 1)
    for c in first:
        c.start()
    for c in first:
        c.wait()
    for k in range(3):
        wide[k, pl.ds(0, cells), :] = halo[0, k]
        wide[k, pl.ds(cells, cells), :] = data[k]
        wide[k, pl.ds(2 * cells, cells), :] = halo[1, k]
    live_wide[pl.ds(0, cells), :] = halo[0, 3]
    live_wide[pl.ds(cells, cells), :] = data[3]
    live_wide[pl.ds(2 * cells, cells), :] = halo[1, 3]
    used = jnp.concatenate([halo[0, 4], data[4], halo[1, 4]], axis=0)
    bars = [
        jnp.broadcast_to((used[:, o : o + 1] - 1.0) * FAR, (ext, LANES)) for o in range(SPAN)
    ]
    for r in range(SPAN):
        bar = zero
        for o in range(SPAN):
            bar = jnp.where((cell_id + (o + SPAN - GHOST)) % SPAN == r, bars[o], bar)
        put(right_rows, ONES + 3 + r, bar)

    low = cells - 2 * GHOST
    diagonal = lax.broadcasted_iota(jnp.int32, (LANES, LANES), 0) == lax.broadcasted_iota(
        jnp.int32, (LANES, LANES), 1
    )
    spring_const = spring_ref[0]
    own = pl.ds(cells, cells)

    def step(it, carry):
        par = lax.rem(it, 2)
        for k in range(3):
            usend[par, k] = wide[k, own, :]
        ucopy = [
            remote(usend.at[par], urecv.at[par, 0], us.at[par, 0], ur.at[par, 0], {"image": down}),
            remote(usend.at[par], urecv.at[par, 1], us.at[par, 1], ur.at[par, 1], {"image": up}),
        ]
        for c in ucopy:
            c.start()

        live = live_wide[...]
        place = [(wide[k] + site[k]) * (1.0 / RADIUS) for k in range(3)]
        for k in range(3):
            h, m, l = parts(place[k])
            for j, v in enumerate((h, h, m, m, h, l)):
                put(left_rows, 6 * k + j, v)
            h, m, l = 2.0 * h, 2.0 * m, 2.0 * l
            for j, v in enumerate((h, m, h, m, l, h)):
                put(right_rows, 6 * k + j, v)
        square = place[0] * place[0] + place[1] * place[1] + place[2] * place[2]
        q = 0.5 - square + (live - 1.0) * FAR
        for j, v in enumerate(parts(q)):
            put(left_rows, ONES - 3 + j, v)
            put(right_rows, ONES + j, v)

        for e in range(low, ext - low):
            block = left_rows[pl.ds(e, ROWS, stride=ext), :]
            flat[:, pl.ds(e * LANES, LANES)] = block.astype(jnp.bfloat16)
            turned[pl.ds((e - low) * LANES, LANES), :] = block.T.astype(jnp.bfloat16)

        for c in range(cells - GHOST, 2 * cells + GHOST):
            near = right_rows[pl.ds(c, ROWS, stride=ext), :].astype(jnp.bfloat16)
            t = jnp.dot(
                turned[pl.ds((c - GHOST - low) * LANES, SPAN * LANES), :], near,
                preferred_element_type=jnp.float32,
            )
            t = jnp.maximum(t, 0.0)
            a, b = GHOST * LANES, (GHOST + 1) * LANES
            t = jnp.concatenate([t[:a], jnp.where(diagonal, 0.0, t[a:b]), t[b:]], axis=0)
            if cells <= c < 2 * cells:
                tiles[c - cells] = t
            s = t * t
            s = s * s
            density[pl.ds(c, 1), :] = jnp.sum(s, axis=0, keepdims=True)

        def lanes(x, y):
            v = x[0] * y[0] + x[1] * y[1] + x[2] * y[2]
            return jnp.sum(v, axis=0, keepdims=True)

        def spread(send, recv, ssem, rsem, rows):
            for j, v in enumerate(rows):
                send[par, pl.ds(j, 1), :] = v
                recv[par, me, pl.ds(j, 1), :] = v
            copies = []
            for d in range(1, n):
                copies.append(
                    remote(
                        send.at[par], recv.at[par, me], ssem.at[par, d], rsem.at[par, d],
                        sp(lax.rem(me + d, n)),
                    )
                )
                copies[-1].start()
            return copies

        steep = 2.0 * live / jnp.sqrt(1.0 + density[...])
        for j, v in enumerate(parts(steep)):
            put(pleft, j, v)
            put(pright, 3 + j, v)
        for e in range(cells - GHOST, 2 * cells + GHOST):
            block = pleft[pl.ds(e, PROWS, stride=ext), :]
            pturned[pl.ds((e - cells + GHOST) * LANES, LANES), :] = block.T.astype(jnp.bfloat16)
        for c in range(cells):
            if c == cells - 1:
                for copy in ucopy:
                    copy.wait_recv()
                own_live = live_wide[own, :]
                ahead, behind = [], []
                for k in range(3):
                    mine = wide[k, own, :]
                    prev = jnp.where(im == 0, data[5 + k], urecv[par, 0, k])
                    nxt = jnp.where(im == ni - 1, data[8 + k], urecv[par, 1, k])
                    ahead.append((nxt - mine) * own_live)
                    behind.append((mine - prev) * own_live)
                    gsend[par, k] = ahead[k]
                    gsend[par, 3 + k] = behind[k]
                gcopy = [
                    remote(gsend.at[par], grecv.at[par, 0], gs.at[par, 0], gr.at[par, 0], sp(right)),
                    remote(gsend.at[par], grecv.at[par, 1], gs.at[par, 1], gr.at[par, 1], sp(left)),
                ]

                acopy = spread(
                    asend, arecv, as_, ar,
                    [lanes(ahead, ahead), lanes(behind, behind), lanes(ahead, behind), own_live[:1]],
                )
                for copy in gcopy:
                    copy.start()
            near = pright[pl.ds(c + cells, PROWS, stride=ext), :].astype(jnp.bfloat16)
            both = jnp.dot(
                pturned[pl.ds(c * LANES, SPAN * LANES), :], near,
                preferred_element_type=jnp.float32,
            )
            t = tiles[c]
            pull = (t * t) * (both * t - 1.2)
            high = pull.astype(jnp.bfloat16)
            rest = (pull - high.astype(jnp.float32)).astype(jnp.bfloat16)
            x = flat[:, pl.ds((c + cells - GHOST) * LANES, SPAN * LANES)]
            v = jnp.dot(x, high, preferred_element_type=jnp.float32) + jnp.dot(
                x, rest, preferred_element_type=jnp.float32
            )
            for k in range(3):
                moment[k, pl.ds(c, 1), :] = (
                    v[6 * k : 6 * k + 1] + v[6 * k + 2 : 6 * k + 3] + v[6 * k + 5 : 6 * k + 6]
                )
            moment[3, pl.ds(c, 1), :] = v[ONES : ONES + 1]

        total = moment[3]
        force = [
            (moment[k] - place[k][cells : 2 * cells] * total) * (2.0 / RADIUS) for k in range(3)
        ]
        for k in range(3):
            fsend[par, k] = force[k]
        bcopy = spread(bsend, brecv, bs, br, [lanes(force, ahead), lanes(force, behind)])
        fcopy = [
            remote(fsend.at[par], frecv.at[par, 0], fs.at[par, 0], fr.at[par, 0], sp(right)),
            remote(fsend.at[par], frecv.at[par, 1], fs.at[par, 1], fr.at[par, 1], sp(left)),
        ]
        for c in fcopy:
            c.start()

        for c in acopy:
            c.wait_recv()
        sums = jnp.sum(jnp.sum(arecv[par], axis=0), axis=-1, keepdims=True)
        aa, bb, ab = sums[0:1], sums[1:2], sums[2:3]
        la, lb = jnp.sqrt(aa + EPS), jnp.sqrt(bb + EPS)
        cosine = ab / (la * lb)
        norm = jnp.sqrt(jnp.maximum(aa / (la * la) + bb / (lb * lb) + 2.0 * cosine, 1.0))
        ga, gb = 1.0 / (la * norm), 1.0 / (lb * norm)
        spring = spring_const * (la - lb)
        for c in gcopy:
            c.wait_recv()
        for c in fcopy:
            c.wait_recv()
        for c in bcopy:
            c.wait_recv()
        sums = jnp.sum(jnp.sum(brecv[par], axis=0), axis=-1, keepdims=True)
        parallel = sums[0:1] * ga + sums[1:2] * gb
        gain = spring - parallel
        ga, gb = gain * ga, gain * gb
        for k in range(3):
            band = force[k] + (ahead[k] * ga + behind[k] * gb)
            out[k] = band
            wide[k, own, :] = wide[k, own, :] + STEP * band
            for side in range(2):
                where = pl.ds(2 * cells * side, cells)
                band = frecv[par, side, k] + (
                    grecv[par, side, k] * ga + grecv[par, side, 3 + k] * gb
                )
                wide[k, where, :] = wide[k, where, :] + STEP * band
        stats[:, 0:1] = parallel
        stats[:, 1:2] = spring
        stats[:, 2:3] = cosine
        for c in ucopy + gcopy + acopy + bcopy + fcopy:
            c.wait_send()
        return carry

    lax.fori_loop(0, ITERATIONS, step, 0)


def solution(mesh):
    n, ni = mesh.shape["space"], mesh.shape["image"]

    def body(displacement, end_states, atom_live, partner_cells, partner_live, spring_const):
        cells = partner_cells.shape[0]
        ext = 3 * cells
        f32, bf16 = jnp.float32, jnp.bfloat16
        sem = pltpu.SemaphoreType.DMA
        V = pltpu.VMEM
        inner = cells + 2 * GHOST
        band, stats = pl.pallas_call(
            functools.partial(kernel, n, ni, cells),
            out_shape=(
                jax.ShapeDtypeStruct((3, cells, LANES), f32),
                jax.ShapeDtypeStruct((1, 3), f32),
            ),
            in_specs=[pl.BlockSpec(memory_space=pltpu.VMEM)] * 5
            + [pl.BlockSpec(memory_space=pltpu.SMEM)],
            out_specs=(pl.BlockSpec(memory_space=pltpu.VMEM),) * 2,
            scratch_shapes=[
                V((11, cells, LANES), f32),
                V((3, ext, LANES), f32),
                V((ext, LANES), f32),
                V((ROWS * ext, LANES), f32),
                V((ROWS * ext, LANES), f32),
                V((PROWS * ext, LANES), f32),
                V((PROWS * ext, LANES), f32),
                V((ROWS, ext * LANES), bf16),
                V(((inner + 2 * GHOST) * LANES, ROWS), bf16),
                V((inner * LANES, PROWS), bf16),
                V((cells, SPAN * LANES, LANES), f32),
                V((ext, LANES), f32),
                V((4, cells, LANES), f32),
                V((2, 5, cells, LANES), f32),
                V((2, 3, cells, LANES), f32),
                V((2, 2, 3, cells, LANES), f32),
                V((2, 6, cells, LANES), f32),
                V((2, 2, 6, cells, LANES), f32),
                V((2, 3, cells, LANES), f32),
                V((2, 2, 3, cells, LANES), f32),
                V((2, 4, LANES), f32),
                V((2, n, 4, LANES), f32),
                V((2, 2, LANES), f32),
                V((2, n, 2, LANES), f32),
                sem((2,)), sem((2,)),
                sem((2, 2)), sem((2, 2)),
                sem((2, 2)), sem((2, 2)),
                sem((2, 2)), sem((2, 2)),
                sem((2, n)), sem((2, n)),
                sem((2, n)), sem((2, n)),
            ],
            compiler_params=pltpu.CompilerParams(collective_id=0, has_side_effects=True),
        )(
            displacement.reshape(3, cells, LANES),
            end_states.reshape(2, 3, cells, LANES).transpose(1, 2, 0, 3).reshape(3, -1, LANES),
            atom_live.reshape(cells, LANES),
            partner_cells, partner_live, spring_const,
        )
        return band.reshape(1, 3, -1), stats

    return jax.shard_map(
        body,
        mesh=mesh,
        in_specs=(
            P("image", None, "space"),
            P(None, None, "space"),
            P("space"),
            P("space", None),
            P("space", None),
            P("image"),
        ),
        out_specs=(P("image", None, "space"), P("image", None)),
        check_vma=False,
    )
```
